256 devices in a mesh: seq: 16 (over y, z_lo), exp: 8 (over x, core), dp: 2 (over z_hi).
Axes of the slice: x: 4, y: 4, z: 8 (z_hi: 2, z_lo: 4; z = z_hi * 4 + z_lo), core: 2. Of those that a mesh axis runs over, the one named last changes fastest.
Arguments:
- queries: bfloat16 [6144, 48, 128], P(('dp', 'seq'), 'exp'), parts along dimension 0, may hold values from -4.5 to 4.5
- keys: bfloat16 [6144, 8, 128], P(('dp', 'seq'), 'exp'), parts along dimension 0, may hold values from -4.5 to 4.5
- values: bfloat16 [6144, 8, 128], P(('dp', 'seq'), 'exp'), parts along dimension 0, may hold values from -16 to 16
- doc_ids: int32 [6144], P('dp'), parts along dimension 0, may hold values from 0 to 2, never falling along the last dimension, each value on 1 to 2560 neighbouring positions
- norm_gain: float32 [6144], replicated, may hold values from 0.1 to 1.9
- expert_ids: int32 [6144, 2], P(('dp', 'seq', 'exp')), parts along dimension 0, may hold values from 0 to 7, all different within a row; in each aligned block of 24 rows (0 to 23, 24 to 47, ...) at most 8 rows name the same one
- route_weights: float32 [6144, 2], P(('dp', 'seq', 'exp')), parts along dimension 0, may hold values from 0.2 to 1
- w_in: bfloat16 [8, 6144, 8192], P('exp', None, 'seq'), may hold values from -0.078125 to 0.078125
- w_out: bfloat16 [8, 8192, 6144], P('exp', 'seq'), may hold values from -0.0625 to 0.0625
Outputs:
- mixed: bfloat16 [6144, 6144], P(('dp', 'seq', 'exp')), parts along dimension 0
The draws below stay inside these ranges and needn't reach their ends.
There are 2 independent parts, one for each index of `dp`. The reference program is written for one: setup_inputs(seed, part) draws one part's arguments, and reference() takes and returns one part's arrays. A program takes and returns all parts, laid end to end along the dimension named above; an argument that names none is the same for every part. Nothing has to cross between parts.
Inputs may be any that keep to these rules, and one draw needn't show every extreme that they name: `doc_ids`: never falling along the sequence. `expert_ids`: within the 24 tokens of one device no expert is named by more than 8 tokens, and in every draw some expert of some device is named by exactly 8; the two experts of a token differ.
All inputs are finite; a program needn't handle non-finite values.
Results may differ from the reference program's by a relative error of at most 0.015.
Values may be sent and summed in bfloat16 or wider, within the bound.
A program may use at most 128 MiB of HBM per device.

```python
import math
import jax
import jax.numpy as jnp
import numpy as np
from jax import lax

HEAD = 128
QH_DEV = 6
HEADS = 48
KV_HEADS = 8
D = 6144
EXPERTS = 8
FF_DEV = 512
FFW = 8192
TOK = 24
SEQ_BLK = 192
TOKENS = 3072
CAP = 8
WINDOW = 2048
NDOC = 3
N_SEQ = 16


def draw_keys(key, part):
    drawn = jnp.clip(jax.random.normal(jax.random.fold_in(key, 3), (TOKENS, KV_HEADS, HEAD), jnp.float32), -4.5, 4.5)
    return drawn.astype(jnp.bfloat16)


def draw_queries(key, part):
    drawn = jnp.clip(jax.random.normal(jax.random.fold_in(key, 5), (TOKENS, HEADS, HEAD), jnp.float32), -4.5, 4.5)
    return drawn.astype(jnp.bfloat16)


def level_of(key, dims, pieces, least, high):
    def one(dim, shards_of):
        draws = jax.random.uniform(jax.random.fold_in(jax.random.fold_in(key, 6), dim), (shards_of,), jnp.float32, least / len(pieces), high / len(pieces))
        return jnp.repeat(jnp.exp(draws), dims[dim] // shards_of).reshape((-1,) + (1,) * (len(dims) - dim - 1))

    loudness = one(*pieces[0])
    for cut in pieces[1:]:
        loudness = loudness * one(*cut)
    return loudness


def profile(count, total, reach, slope):
    loads = [(1 << 20) // math.isqrt(standing ** slope) + 1 for standing in range(2, count + 1)]
    rest, holding = total - reach - (count - 1), [1] * (count - 1)
    while rest > 0:
        candidates = [i for i in range(count - 1) if holding[i] < reach]
        mass, budget = sum([loads[i] for i in candidates]), rest
        for i in candidates:
            more = min(reach - holding[i], max(1, budget * loads[i] // mass), rest)
            holding[i] = holding[i] + more
            rest = rest - more
    return np.array([reach] + holding)


def uneven(key, number_of, total, reach, skew):
    if number_of == 2:
        one = jax.random.randint(key, (), max(1, total - reach), min(reach, total - 1) + 1)
        return jnp.stack([one, total - one])
    sizes = jnp.asarray(profile(number_of, total, reach, skew), jnp.int32)
    couples = (number_of - 1) // 2
    giver, sink = sizes[1:1 + 2 * couples:2], sizes[2:2 + 2 * couples:2]
    slack = jnp.minimum(giver - 1, reach - sink)
    passed = jax.random.randint(jax.random.fold_in(key, 1), (couples,), 0, 1 << 20) % (slack + 1)
    sizes = sizes.at[1:1 + 2 * couples:2].set(giver - passed).at[2:2 + 2 * couples:2].set(sink + passed)
    return sizes[jax.random.permutation(jax.random.fold_in(key, 2), number_of)]


def routed_block(key, own, number, rows, amount, top, bound, skew):
    ranking = jax.random.permutation(key, amount)
    heavy_load, common = load_shares(amount, rows * top, bound, skew, True), load_shares(amount, rows * top, bound, skew, False)
    places = jnp.arange(amount)

    def named(lengths, turn):
        used = int((lengths > 0).sum())
        fixed = max(1, used // 4)
        shifted = fixed + (places - fixed + turn * (used - fixed)) % max(1, amount - fixed)
        return jnp.zeros((amount,), jnp.int32).at[ranking[jnp.where(places < fixed, places, shifted)]].set(jnp.asarray(lengths, jnp.int32))

    lengths = jnp.where(number % 4 == 0, named(heavy_load, number // 4), named(common, number - number // 4 - 1))
    mixed = jax.random.permutation(jax.random.fold_in(own, 3), amount)
    donor, sink = mixed[0:amount // 2 * 2:2], mixed[1:amount // 2 * 2:2]
    slack = jnp.minimum(lengths[donor] - 1, bound - lengths[sink]) // 2
    slack = jnp.where((donor == ranking[0]) | (sink == ranking[0]) | (lengths[sink] == 0), 0, jnp.maximum(slack, 0))
    shifted = jax.random.randint(jax.random.fold_in(own, 4), (amount // 2,), 0, 1 << 20) % (slack + 1)
    lengths = lengths.at[donor].add(-shifted).at[sink].add(shifted)
    labels = jnp.searchsorted(jnp.cumsum(lengths), jnp.arange(rows * top), side="right").astype(jnp.int32)
    listing = labels.reshape(top, rows).T
    listing = listing[jax.random.permutation(jax.random.fold_in(own, 1), rows)]
    turn = jax.random.randint(jax.random.fold_in(own, 2), (rows, 1), 0, top)
    return jnp.take_along_axis(listing, (jnp.arange(top)[None, :] + turn) % top, axis=1)


def load_shares(count, total, bound, slope, full):
    portions = [(1 << 20) // math.isqrt(standing ** slope) + 1 for standing in range(1, count + 1)]
    largest = bound if full else min(bound, max(-(-total // count), total * portions[0] // sum(portions)))
    least = 1 if total - largest >= count - 1 else 0
    counts, surplus = [largest] + [least] * (count - 1), total - largest - least * (count - 1)
    while surplus > 0:
        free = [i for i in range(1, count) if counts[i] < largest] or [i for i in range(1, count) if counts[i] < bound]
        pool, remaining = sum([portions[i] for i in free]), surplus
        for i in free:
            more = min(bound - counts[i], max(1, remaining * portions[i] // pool), surplus)
            counts[i] = counts[i] + more
            surplus = surplus - more
    return np.array(counts)


def gaussian(key, shape, spread, limit, split=(), kind=jnp.bfloat16):
    factor_of = level_of(key, shape, split, -0.22, 0.18) if split else 1.0
    result = jax.random.normal(key, shape, jnp.float32) * spread * factor_of
    return jnp.minimum(jnp.maximum(result, -limit), limit).astype(kind)


def setup_inputs(seed: int = 0, part: int = 0) -> dict:
    streams_of = jax.random.split(jax.random.key(seed), 10)
    own_keys = jax.random.split(jax.random.fold_in(streams_of[9], part), 10)
    queries = draw_queries(jax.random.fold_in(jax.random.fold_in(streams_of[9], part), 71), part)
    keys = draw_keys(jax.random.fold_in(jax.random.fold_in(streams_of[9], part), 71), part)
    values = gaussian(own_keys[2], (TOKENS, KV_HEADS, HEAD), 4.0, 16.0, ((0, 16), (1, 8)))
    doc_ids = jnp.searchsorted(jnp.cumsum(uneven(own_keys[3], NDOC, TOKENS, TOKENS * 5 // 6, 0)), jnp.arange(TOKENS), side="right").astype(jnp.int32)
    norm_gain = jnp.clip(1.0 + 0.18 * jax.random.normal(streams_of[4], (D,), jnp.float32), 0.1, 1.9)
    expert_ids_keys = jax.random.split(jax.random.fold_in(own_keys[5], 1), TOKENS // TOK)
    expert_ids_turns = jax.random.permutation(jax.random.fold_in(own_keys[5], 3), TOKENS // TOK)
    expert_ids = jax.vmap(lambda own, number: routed_block(jax.random.fold_in(own_keys[5], 2), own, number, TOK, EXPERTS, 2, CAP, 2))(expert_ids_keys, expert_ids_turns).reshape((TOKENS, 2))
    route_weights = jnp.clip(0.2 + 0.8 * jax.random.uniform(own_keys[6], (TOKENS, 2), jnp.float32) ** level_of(own_keys[6], (TOKENS, 2), ((0, 128),), -0.2, 0.2), 0.2, 1.0)
    w_in = gaussian(streams_of[7], (EXPERTS, D, FFW), D ** -0.5, 0.078125, ((0, 8), (2, 16)))
    w_out = gaussian(streams_of[8], (EXPERTS, FFW, D), FFW ** -0.5, 0.0625, ((0, 8), (1, 16)))
    return {"queries": queries, "keys": keys, "values": values, "doc_ids": doc_ids, "norm_gain": norm_gain, "expert_ids": expert_ids, "route_weights": route_weights, "w_in": w_in, "w_out": w_out}


epsilon = 1e-05

def attend_block(block_index, queries, keys, values, doc_ids):
    start = block_index * SEQ_BLK
    query_block = lax.dynamic_slice_in_dim(queries, start, SEQ_BLK, 0).astype(jnp.float32)
    query_block = query_block.reshape(SEQ_BLK, KV_HEADS, QH_DEV, HEAD)
    key_float = keys.astype(jnp.float32)
    value_float = values.astype(jnp.float32)
    score = jnp.einsum('bgqe,tge->gqbt', query_block, key_float) * (1.0 / HEAD ** 0.5)
    query_pos = start + jnp.arange(SEQ_BLK, dtype=jnp.int32)
    key_pos = jnp.arange(TOKENS, dtype=jnp.int32)
    query_doc = lax.dynamic_slice_in_dim(doc_ids, start, SEQ_BLK, 0)
    allowed = (key_pos[None, :] <= query_pos[:, None]) & (query_pos[:, None] - key_pos[None, :] < WINDOW)
    allowed = allowed & (query_doc[:, None] == doc_ids[None, :])
    score = jnp.where(allowed[None, None], score, -jnp.inf)
    top_score = lax.optimization_barrier(jnp.max(score, axis=3, keepdims=True))
    weights = jnp.where(allowed[None, None], jnp.exp(score - top_score), 0.0)
    probs = (weights / lax.optimization_barrier(jnp.sum(weights, axis=3, keepdims=True))).astype(jnp.bfloat16)
    output = jnp.einsum('gqbt,tge->bgqe', probs.astype(jnp.float32), value_float)
    return output.reshape(SEQ_BLK, D).astype(jnp.bfloat16)

def reference(queries, keys, values, doc_ids, norm_gain, expert_ids, route_weights, w_in, w_out):
    attn = lax.map(lambda index: attend_block(index, queries, keys, values, doc_ids), jnp.arange(N_SEQ, dtype=jnp.int32))
    attn = attn.reshape(TOKENS, D)
    attn_float = attn.astype(jnp.float32)
    mean_square = lax.optimization_barrier(jnp.mean(attn_float * attn_float, axis=1, keepdims=True))
    normed = (attn_float * lax.rsqrt(mean_square + epsilon) * norm_gain[None, :]).astype(jnp.bfloat16)
    run_count = TOKENS // TOK
    flat_ids = expert_ids.reshape(run_count, TOK * 2)
    onehot = (flat_ids[:, :, None] == jnp.arange(EXPERTS, dtype=jnp.int32)[None, None, :]).astype(jnp.int32)
    earlier = jnp.cumsum(onehot, axis=1) - onehot
    slot = lax.optimization_barrier(jnp.sum(earlier * onehot, axis=2))
    row_code = (jnp.arange(run_count, dtype=jnp.int32)[:, None] * CAP + slot).reshape(TOKENS, 2)
    token_code = jnp.arange(TOKENS, dtype=jnp.int32)[:, None] + jnp.zeros((1, 2), jnp.int32)
    table = jnp.zeros((EXPERTS, run_count * CAP), jnp.int32).at[expert_ids, row_code].set(token_code + 1)
    padded = jnp.concatenate([jnp.zeros((1, D), jnp.bfloat16), normed], axis=0)

    def run_expert(expert):
        rows = padded[table[expert]]
        hidden = jax.nn.silu(jnp.dot(rows, w_in[expert], preferred_element_type=jnp.float32)).astype(jnp.bfloat16)
        out_weight = w_out[expert]

        def add_slice(total, index):
            hidden_part = lax.dynamic_slice_in_dim(hidden, index * FF_DEV, FF_DEV, 1)
            weight_part = lax.dynamic_slice_in_dim(out_weight, index * FF_DEV, FF_DEV, 0)
            partial_value = jnp.dot(hidden_part, weight_part, preferred_element_type=jnp.float32).astype(jnp.bfloat16)
            partial_value = lax.optimization_barrier(partial_value)
            return (total + partial_value.astype(jnp.float32), None)
        total, unused = lax.scan(add_slice, jnp.zeros((run_count * CAP, D), jnp.float32), jnp.arange(N_SEQ, dtype=jnp.int32))
        return total.astype(jnp.bfloat16)
    expert_out = lax.map(run_expert, jnp.arange(EXPERTS, dtype=jnp.int32))
    picked = expert_out[expert_ids, row_code].astype(jnp.float32)
    mixed = attn_float + route_weights[:, 0:1] * picked[:, 0] + route_weights[:, 1:2] * picked[:, 1]
    return mixed.astype(jnp.bfloat16)
```

```python
import functools

import jax
import jax.numpy as jnp
from jax import lax
from jax.experimental import pallas as pl
from jax.experimental.pallas import tpu as pltpu
from jax.sharding import PartitionSpec as P

WINDOW = 2048
EXP = 8
NY = 4
NZ = 4
CAP = 8
ROWS = EXP * CAP
HALF = ROWS // 2

epsilon = 1e-05


def shifted(x, axis, by):
    size = lax.axis_size(axis)
    pairs = [(i, i + by) for i in range(size) if 0 <= i + by < size]
    return lax.ppermute(x, axis, pairs)


def moe_kernel(
    going, w_in, w_out, result,
    arrived, rows, hidden, part, halves, sides, quads, leaving, back, wi, wo,
    w_sem, x_send, x_recv, z_send, z_recv, y_send, y_recv, h_send, h_recv,
    a_send, a_recv, b_send, b_recv, q_send, q_recv, r_send, r_recv,
):
    seq = lax.axis_index("seq")
    exp = lax.axis_index("exp")
    y = seq // NZ
    z = seq % NZ
    y_up = (y + 1) % NY
    y_down = (y + NY - 1) % NY
    y_far = (y + 2) % NY
    up = {"seq": y_up * NZ + z}
    down = {"seq": y_down * NZ + z}
    column = [z, z + 1 - 2 * (z % 2), 2 - z // 2, 3 - 3 * (z // 2)]
    width = rows.shape[2]

    load_in = pltpu.make_async_copy(w_in, wi, w_sem.at[0])
    load_out = pltpu.make_async_copy(w_out, wo, w_sem.at[1])
    load_in.start()
    load_out.start()

    barrier = pltpu.get_barrier_semaphore()
    greeted = [up, down]
    greeted += [{"seq": y * NZ + column[k]} for k in range(1, NZ)]
    greeted += [{"exp": (exp + d) % EXP} for d in range(1, EXP)]
    for device in greeted:
        pl.semaphore_signal(barrier, inc=1, device_id=device, device_id_type=pl.DeviceIdType.MESH)
    pl.semaphore_wait(barrier, len(greeted))

    sent = []

    def copy(src, dst, send, recv, device):
        return pltpu.make_async_remote_copy(
            src_ref=src, dst_ref=dst, send_sem=send, recv_sem=recv,
            device_id=device, device_id_type=pl.DeviceIdType.MESH,
        )

    def push(src, dst, send, recv, device):
        started = copy(src, dst, send, recv, device)
        started.start()
        sent.append(started)

    def arrive(dst, send, recv):
        copy(dst, dst, send, recv, up).wait_recv()

    def block(col, yy):
        return rows.at[col, pl.ds(pl.multiple_of(yy * ROWS, ROWS), ROWS)]

    def half_block(col, yy, h):
        return rows.at[col, pl.ds(pl.multiple_of(yy * ROWS + h * HALF, HALF), HALF)]

    def part_block(k, yy):
        return part.at[k, pl.ds(pl.multiple_of(yy * ROWS, ROWS), ROWS)]

    def part_half(k, yy, h):
        return part.at[k, pl.ds(pl.multiple_of(yy * ROWS + h * HALF, HALF), HALF)]

    for d in range(1, EXP):
        other = (exp + d) % EXP
        push(going.at[other], arrived.at[exp], x_send.at[d - 1], x_recv.at[d - 1], {"exp": other})
    arrived[exp] = going[exp]
    for d in range(1, EXP):
        source = (exp + EXP - d) % EXP
        arrive(arrived.at[source], x_send.at[d - 1], x_recv.at[d - 1])
    own_rows = block(z, y)
    own_rows[...] = arrived[...].reshape(ROWS, width)

    def gather_send(k):
        if k > 0:
            arrive(block(column[k], y), z_send.at[k - 1], z_recv.at[column[k]])
        ref = block(column[k], y)
        push(ref, ref, y_send.at[k, 0], y_recv.at[k, 0], up)
        push(ref, ref, y_send.at[k, 1], y_recv.at[k, 1], down)

    def gather_pass(k):
        arrive(block(column[k], y_down), y_send.at[k, 0], y_recv.at[k, 0])
        ref = half_block(column[k], y_down, 0)
        push(ref, ref, h_send.at[k, 0], h_recv.at[k, 0], up)
        arrive(block(column[k], y_up), y_send.at[k, 1], y_recv.at[k, 1])
        ref = half_block(column[k], y_up, 1)
        push(ref, ref, h_send.at[k, 1], h_recv.at[k, 1], down)

    def compute(k):
        for h in range(2):
            arrive(half_block(column[k], y_far, h), h_send.at[k, h], h_recv.at[k, h])
        if k == 0:
            load_in.wait()
        rows_now = rows.at[column[k]]

        @pl.loop(0, wi.shape[1] // 256)
        def _(n):
            cols = pl.ds(pl.multiple_of(n * 256, 256), 256)
            v = jnp.dot(rows_now[...], wi[:, cols], preferred_element_type=jnp.float32)
            hidden[:, cols] = (v / (1.0 + jnp.exp(-v))).astype(jnp.bfloat16)

        if k == 0:
            load_out.wait()

        @pl.loop(0, width // 512)
        def _(n):
            cols = pl.ds(pl.multiple_of(n * 512, 512), 512)
            part[k, :, cols] = jnp.dot(
                hidden[...], wo[:, cols], preferred_element_type=jnp.float32
            ).astype(jnp.bfloat16)

    def reduce_far(k):
        push(part_half(k, y_far, 0), halves.at[k, 0], a_send.at[k, 0], a_recv.at[k, 0], up)
        push(part_half(k, y_far, 1), halves.at[k, 1], a_send.at[k, 1], a_recv.at[k, 1], down)

    def reduce_near(k):
        for h, yy, device in ((0, y_up, up), (1, y_down, down)):
            arrive(halves.at[k, h], a_send.at[k, h], a_recv.at[k, h])
            target = part_half(k, yy, h)

            @pl.loop(0, width // 1024)
            def _(n):
                cols = pl.ds(pl.multiple_of(n * 1024, 1024), 1024)
                target[:, cols] = (
                    target[:, cols].astype(jnp.float32) + halves[k, h, :, cols].astype(jnp.float32)
                ).astype(jnp.bfloat16)

            push(part_block(k, yy), sides.at[k, h], b_send.at[k, h], b_recv.at[k, h], device)

    def reduce_own(k):
        for h in range(2):
            arrive(sides.at[k, h], b_send.at[k, h], b_recv.at[k, h])
        if k == 0:
            return
        target = part_block(k, y)

        @pl.loop(0, width // 512)
        def _(n):
            cols = pl.ds(pl.multiple_of(n * 512, 512), 512)
            target[:, cols] = (
                target[:, cols].astype(jnp.float32)
                + sides[k, 0, :, cols].astype(jnp.float32)
                + sides[k, 1, :, cols].astype(jnp.float32)
            ).astype(jnp.bfloat16)

        push(target, quads.at[z], q_send.at[k - 1], q_recv.at[z], {"seq": y * NZ + column[k]})

    for k in range(1, NZ):
        push(own_rows, own_rows, z_send.at[k - 1], z_recv.at[z], {"seq": y * NZ + column[k]})
    gather_send(0)
    gather_send(1)
    gather_pass(0)
    gather_send(2)
    gather_pass(1)
    compute(0)
    gather_send(3)
    gather_pass(2)
    compute(1)
    reduce_far(1)
    gather_pass(3)
    compute(2)
    reduce_far(2)
    reduce_near(1)
    compute(3)
    reduce_far(3)
    reduce_near(2)
    reduce_own(1)
    reduce_far(0)
    reduce_near(3)
    reduce_own(2)
    reduce_near(0)
    reduce_own(3)
    reduce_own(0)
    for k in range(1, NZ):
        arrive(quads.at[column[k]], q_send.at[k - 1], q_recv.at[column[k]])
    mine = part_block(0, y)

    @pl.loop(0, width // 512)
    def _(n):
        cols = pl.ds(pl.multiple_of(n * 512, 512), 512)
        total = (
            mine[:, cols].astype(jnp.float32)
            + sides[0, 0, :, cols].astype(jnp.float32)
            + sides[0, 1, :, cols].astype(jnp.float32)
        )
        for k in range(1, NZ):
            total = total + quads[column[k], :, cols].astype(jnp.float32)
        leaving[:, :, cols] = total.astype(jnp.bfloat16).reshape(EXP, CAP, 512)

    for d in range(1, EXP):
        other = (exp + d) % EXP
        push(leaving.at[other], back.at[exp], r_send.at[d - 1], r_recv.at[d - 1], {"exp": other})
    back[exp] = leaving[exp]
    for d in range(1, EXP):
        source = (exp + EXP - d) % EXP
        arrive(back.at[source], r_send.at[d - 1], r_recv.at[d - 1])
    result[...] = back[...].reshape(ROWS, width)
    for started in sent:
        started.wait_send()


def experts(going, w_in, w_out):
    width, ff = w_in.shape
    dma = pltpu.SemaphoreType.DMA
    b16 = jnp.bfloat16
    vmem = pltpu.VMEM
    return pl.pallas_call(
        moe_kernel,
        out_shape=jax.ShapeDtypeStruct((ROWS, width), b16),
        in_specs=[
            pl.BlockSpec(memory_space=pltpu.VMEM),
            pl.BlockSpec(memory_space=pl.ANY),
            pl.BlockSpec(memory_space=pl.ANY),
        ],
        out_specs=pl.BlockSpec(memory_space=pltpu.VMEM),
        scratch_shapes=[
            vmem((EXP, CAP, width), b16),
            vmem((NZ, NY * ROWS, width), b16),
            vmem((NY * ROWS, ff), b16),
            vmem((NZ, NY * ROWS, width), b16),
            vmem((NZ, 2, HALF, width), b16),
            vmem((NZ, 2, ROWS, width), b16),
            vmem((NZ, ROWS, width), b16),
            vmem((EXP, CAP, width), b16),
            vmem((EXP, CAP, width), b16),
            vmem((width, ff), b16),
            vmem((ff, width), b16),
            dma((2,)),
            dma((EXP - 1,)), dma((EXP - 1,)),
            dma((NZ - 1,)), dma((NZ,)),
            dma((NZ, 2)), dma((NZ, 2)),
            dma((NZ, 2)), dma((NZ, 2)),
            dma((NZ, 2)), dma((NZ, 2)),
            dma((NZ, 2)), dma((NZ, 2)),
            dma((NZ - 1,)), dma((NZ,)),
            dma((EXP - 1,)), dma((EXP - 1,)),
        ],
        compiler_params=pltpu.CompilerParams(
            collective_id=0, has_side_effects=True, vmem_limit_bytes=67043328
        ),
    )(going, w_in, w_out)


def shards(queries, keys, values, doc_ids, norm_gain, expert_ids, route_weights, w_in, w_out):
    block_len, heads_dev, head_dim = queries.shape
    seq_count = lax.axis_size("seq")
    exp_count = lax.axis_size("exp")
    seq_index = lax.axis_index("seq")
    reach_blocks = min(-(-WINDOW // block_len), seq_count - 1)
    own_keys = keys[:, 0, :]
    own_values = values[:, 0, :]
    key_list = [own_keys]
    value_list = [own_values]
    for distance in range(1, reach_blocks + 1):
        far_keys, far_values = shifted((own_keys, own_values), "seq", distance)
        key_list.insert(0, far_keys)
        value_list.insert(0, far_values)
    near_keys = jnp.concatenate(key_list, axis=0)
    near_values = jnp.concatenate(value_list, axis=0)
    key_count = near_keys.shape[0]
    query_rows = jnp.transpose(queries, (1, 0, 2)).reshape(heads_dev * block_len, head_dim)
    score = lax.dot_general(
        query_rows, near_keys, (((1,), (1,)), ((), ())), preferred_element_type=jnp.float32
    )
    score = score * (1.0 / head_dim**0.5)
    query_pos = seq_index * block_len + jnp.arange(block_len, dtype=jnp.int32)
    key_pos = (seq_index - reach_blocks) * block_len + jnp.arange(key_count, dtype=jnp.int32)
    padded_docs = jnp.concatenate(
        [jnp.full((reach_blocks * block_len,), -1, jnp.int32), doc_ids], axis=0
    )
    key_docs = lax.dynamic_slice_in_dim(padded_docs, seq_index * block_len, key_count, 0)
    query_docs = lax.dynamic_slice_in_dim(doc_ids, seq_index * block_len, block_len, 0)
    allowed = (key_pos[None, :] <= query_pos[:, None]) & (
        query_pos[:, None] - key_pos[None, :] < WINDOW
    )
    allowed = allowed & (key_pos[None, :] >= 0) & (query_docs[:, None] == key_docs[None, :])
    allowed = jnp.tile(allowed, (heads_dev, 1))
    score = jnp.where(allowed, score, -jnp.inf)
    top_score = jnp.max(score, axis=1, keepdims=True)
    weights = jnp.where(allowed, jnp.exp(score - top_score), 0.0)
    probs = (weights / jnp.sum(weights, axis=1, keepdims=True)).astype(jnp.bfloat16)
    attended = jnp.dot(probs, near_values, preferred_element_type=jnp.float32).astype(jnp.bfloat16)
    attended = jnp.transpose(attended.reshape(heads_dev, block_len, head_dim), (1, 0, 2)).reshape(
        block_len, heads_dev * head_dim
    )
    attn = lax.all_to_all(attended, "exp", split_axis=0, concat_axis=1, tiled=True)
    token_count = attn.shape[0]
    width = attn.shape[1]
    attn_float = attn.astype(jnp.float32)
    mean_square = jnp.mean(attn_float * attn_float, axis=1, keepdims=True)
    normed = (attn_float * lax.rsqrt(mean_square + epsilon) * norm_gain[None, :]).astype(
        jnp.bfloat16
    )
    flat_ids = expert_ids.reshape(token_count * 2)
    onehot = (flat_ids[:, None] == jnp.arange(exp_count, dtype=jnp.int32)[None, :]).astype(
        jnp.int32
    )
    earlier = jnp.cumsum(onehot, axis=0) - onehot
    slot = jnp.sum(earlier * onehot, axis=1)
    local_code = (flat_ids * CAP + slot).reshape(token_count, 2)
    slot_range = jnp.arange(ROWS, dtype=jnp.int32)
    first_hit = local_code[:, 0:1] == slot_range[None, :]
    second_hit = local_code[:, 1:2] == slot_range[None, :]
    placing = jnp.transpose((first_hit | second_hit).astype(jnp.bfloat16))
    outgoing = jnp.dot(placing, normed, preferred_element_type=jnp.float32).astype(jnp.bfloat16)
    returned = experts(outgoing.reshape(EXP, CAP, width), w_in[0], w_out[0])
    combine = route_weights[:, 0:1] * first_hit.astype(jnp.float32) + route_weights[
        :, 1:2
    ] * second_hit.astype(jnp.float32)
    moe_part = jnp.dot(
        combine,
        returned.astype(jnp.float32),
        precision=lax.Precision.HIGHEST,
        preferred_element_type=jnp.float32,
    )
    return (attn_float + moe_part).astype(jnp.bfloat16)


def solution(mesh):
    placed = (
        P(("dp", "seq"), "exp", None),
        P(("dp", "seq"), "exp", None),
        P(("dp", "seq"), "exp", None),
        P("dp"),
        P(),
        P(("dp", "seq", "exp"), None),
        P(("dp", "seq", "exp"), None),
        P("exp", None, "seq"),
        P("exp", "seq", None),
    )
    return jax.shard_map(
        shards, mesh=mesh, in_specs=placed, out_specs=P(("dp", "seq", "exp"), None), check_vma=False
    )
```

```python
import functools

import jax
import jax.numpy as jnp
from jax import lax
from jax.experimental import pallas as pl
from jax.experimental.pallas import tpu as pltpu
from jax.sharding import PartitionSpec as P

WINDOW = 2048
EXP = 8
NY = 4
NZ = 4
CAP = 8
ROWS = EXP * CAP
HALF = ROWS // 2

epsilon = 1e-05


def place_on_torus():
    seq = lax.axis_index("seq")
    y = seq // NZ
    z = seq % NZ
    column = [z, z + 1 - 2 * (z % 2), 2 - z // 2, 3 - 3 * (z // 2)]
    return y, z, column


def context_kernel(
    keys, values, all_keys, all_values, z_send, z_recv, y_send, y_recv, h_send, h_recv
):
    y, z, column = place_on_torus()
    y_up = (y + 1) % NY
    y_down = (y + NY - 1) % NY
    y_far = (y + 2) % NY
    up = {"seq": y_up * NZ + z}
    down = {"seq": y_down * NZ + z}
    length = keys.shape[0]
    half = length // 2

    barrier = pltpu.get_barrier_semaphore()
    greeted = [up, down] + [{"seq": y * NZ + column[k]} for k in range(1, NZ)]
    for device in greeted:
        pl.semaphore_signal(barrier, inc=1, device_id=device, device_id_type=pl.DeviceIdType.MESH)

    def rows_of(ref, col, yy):
        start = (yy * NZ + col) * length
        return ref.at[pl.ds(pl.multiple_of(start, length), length)]

    def half_of(ref, col, yy, h):
        start = (yy * NZ + col) * length + h * half
        return ref.at[pl.ds(pl.multiple_of(start, half), half)]

    both = (all_keys, all_values)
    for own, ref in zip((keys, values), both):
        rows_of(ref, z, y)[...] = own[...]
    pl.semaphore_wait(barrier, len(greeted))
    sent = []

    def copy(ref, send, recv, device):
        return pltpu.make_async_remote_copy(
            src_ref=ref, dst_ref=ref, send_sem=send, recv_sem=recv,
            device_id=device, device_id_type=pl.DeviceIdType.MESH,
        )

    def push(ref, send, recv, device):
        started = copy(ref, send, recv, device)
        started.start()
        sent.append(started)

    for k in range(1, NZ):
        for i, ref in enumerate(both):
            push(
                rows_of(ref, z, y), z_send.at[k - 1, i], z_recv.at[z, i],
                {"seq": y * NZ + column[k]},
            )

    def spread(k):
        for i, ref in enumerate(both):
            block = rows_of(ref, column[k], y)
            if k > 0:
                copy(block, z_send.at[k - 1, i], z_recv.at[column[k], i], up).wait_recv()
            push(block, y_send.at[k, 0, i], y_recv.at[k, 0, i], up)
            push(block, y_send.at[k, 1, i], y_recv.at[k, 1, i], down)

    def pass_on(k):
        for h, yy, device in ((0, y_down, up), (1, y_up, down)):
            for i, ref in enumerate(both):
                block = rows_of(ref, column[k], yy)
                copy(block, y_send.at[k, h, i], y_recv.at[k, h, i], up).wait_recv()
                part = half_of(ref, column[k], yy, h)
                push(part, h_send.at[k, h, i], h_recv.at[k, h, i], device)

    spread(0)
    spread(1)
    pass_on(0)
    spread(2)
    pass_on(1)
    spread(3)
    pass_on(2)
    pass_on(3)
    for k in range(NZ):
        for h in range(2):
            for i, ref in enumerate(both):
                part = half_of(ref, column[k], y_far, h)
                copy(part, h_send.at[k, h, i], h_recv.at[k, h, i], up).wait_recv()
    for started in sent:
        started.wait_send()


def gather_context(keys, values):
    length, head_dim = keys.shape
    dma = pltpu.SemaphoreType.DMA
    whole = jax.ShapeDtypeStruct((NY * NZ * length, head_dim), keys.dtype)
    vmem = pl.BlockSpec(memory_space=pltpu.VMEM)
    return pl.pallas_call(
        context_kernel,
        out_shape=(whole, whole),
        in_specs=[vmem, vmem],
        out_specs=(vmem, vmem),
        scratch_shapes=[
            dma((NZ - 1, 2)), dma((NZ, 2)),
            dma((NZ, 2, 2)), dma((NZ, 2, 2)),
            dma((NZ, 2, 2)), dma((NZ, 2, 2)),
        ],
        compiler_params=pltpu.CompilerParams(collective_id=1, has_side_effects=True),
    )(keys, values)


def moe_kernel(
    going, w_in, w_out, result,
    arrived, rows, hidden, part, halves, sides, quads, leaving, back, wi, wo,
    w_sem, x_send, x_recv, z_send, z_recv, y_send, y_recv, h_send, h_recv,
    a_send, a_recv, b_send, b_recv, q_send, q_recv, r_send, r_recv,
):
    exp = lax.axis_index("exp")
    y, z, column = place_on_torus()
    y_up = (y + 1) % NY
    y_down = (y + NY - 1) % NY
    y_far = (y + 2) % NY
    up = {"seq": y_up * NZ + z}
    down = {"seq": y_down * NZ + z}
    width = rows.shape[2]

    load_in = pltpu.make_async_copy(w_in, wi, w_sem.at[0])
    load_out = pltpu.make_async_copy(w_out, wo, w_sem.at[1])
    load_in.start()
    load_out.start()

    barrier = pltpu.get_barrier_semaphore()
    greeted = [up, down]
    greeted += [{"seq": y * NZ + column[k]} for k in range(1, NZ)]
    greeted += [{"exp": (exp + d) % EXP} for d in range(1, EXP)]
    for device in greeted:
        pl.semaphore_signal(barrier, inc=1, device_id=device, device_id_type=pl.DeviceIdType.MESH)
    pl.semaphore_wait(barrier, len(greeted))

    sent = []

    def copy(src, dst, send, recv, device):
        return pltpu.make_async_remote_copy(
            src_ref=src, dst_ref=dst, send_sem=send, recv_sem=recv,
            device_id=device, device_id_type=pl.DeviceIdType.MESH,
        )

    def push(src, dst, send, recv, device):
        started = copy(src, dst, send, recv, device)
        started.start()
        sent.append(started)

    def arrive(dst, send, recv):
        copy(dst, dst, send, recv, up).wait_recv()

    def block(col, yy):
        return rows.at[col, pl.ds(pl.multiple_of(yy * ROWS, ROWS), ROWS)]

    def half_block(col, yy, h):
        return rows.at[col, pl.ds(pl.multiple_of(yy * ROWS + h * HALF, HALF), HALF)]

    def part_block(k, yy):
        return part.at[k, pl.ds(pl.multiple_of(yy * ROWS, ROWS), ROWS)]

    def part_half(k, yy, h):
        return part.at[k, pl.ds(pl.multiple_of(yy * ROWS + h * HALF, HALF), HALF)]

    for d in range(1, EXP):
        other = (exp + d) % EXP
        push(going.at[other], arrived.at[exp], x_send.at[d - 1], x_recv.at[d - 1], {"exp": other})
    arrived[exp] = going[exp]
    for d in range(1, EXP):
        source = (exp + EXP - d) % EXP
        arrive(arrived.at[source], x_send.at[d - 1], x_recv.at[d - 1])
    own_rows = block(z, y)
    own_rows[...] = arrived[...].reshape(ROWS, width)

    def gather_send(k):
        if k > 0:
            arrive(block(column[k], y), z_send.at[k - 1], z_recv.at[column[k]])
        ref = block(column[k], y)
        push(ref, ref, y_send.at[k, 0], y_recv.at[k, 0], up)
        push(ref, ref, y_send.at[k, 1], y_recv.at[k, 1], down)

    def gather_pass(k):
        arrive(block(column[k], y_down), y_send.at[k, 0], y_recv.at[k, 0])
        ref = half_block(column[k], y_down, 0)
        push(ref, ref, h_send.at[k, 0], h_recv.at[k, 0], up)
        arrive(block(column[k], y_up), y_send.at[k, 1], y_recv.at[k, 1])
        ref = half_block(column[k], y_up, 1)
        push(ref, ref, h_send.at[k, 1], h_recv.at[k, 1], down)

    def compute(k):
        for h in range(2):
            arrive(half_block(column[k], y_far, h), h_send.at[k, h], h_recv.at[k, h])
        if k == 0:
            load_in.wait()
        rows_now = rows.at[column[k]]

        @pl.loop(0, wi.shape[1] // 256)
        def _(n):
            cols = pl.ds(pl.multiple_of(n * 256, 256), 256)
            v = jnp.dot(rows_now[...], wi[:, cols], preferred_element_type=jnp.float32)
            hidden[:, cols] = (v / (1.0 + jnp.exp(-v))).astype(jnp.bfloat16)

        if k == 0:
            load_out.wait()

        @pl.loop(0, width // 512)
        def _(n):
            cols = pl.ds(pl.multiple_of(n * 512, 512), 512)
            part[k, :, cols] = jnp.dot(
                hidden[...], wo[:, cols], preferred_element_type=jnp.float32
            ).astype(jnp.bfloat16)

    def reduce_far(k):
        push(part_half(k, y_far, 0), halves.at[k, 0], a_send.at[k, 0], a_recv.at[k, 0], up)
        push(part_half(k, y_far, 1), halves.at[k, 1], a_send.at[k, 1], a_recv.at[k, 1], down)

    def reduce_near(k):
        for h, yy, device in ((0, y_up, up), (1, y_down, down)):
            arrive(halves.at[k, h], a_send.at[k, h], a_recv.at[k, h])
            target = part_half(k, yy, h)

            @pl.loop(0, width // 1024)
            def _(n):
                cols = pl.ds(pl.multiple_of(n * 1024, 1024), 1024)
                target[:, cols] = (
                    target[:, cols].astype(jnp.float32) + halves[k, h, :, cols].astype(jnp.float32)
                ).astype(jnp.bfloat16)

            push(part_block(k, yy), sides.at[k, h], b_send.at[k, h], b_recv.at[k, h], device)

    def reduce_own(k):
        for h in range(2):
            arrive(sides.at[k, h], b_send.at[k, h], b_recv.at[k, h])
        if k == 0:
            return
        target = part_block(k, y)

        @pl.loop(0, width // 512)
        def _(n):
            cols = pl.ds(pl.multiple_of(n * 512, 512), 512)
            target[:, cols] = (
                target[:, cols].astype(jnp.float32)
                + sides[k, 0, :, cols].astype(jnp.float32)
                + sides[k, 1, :, cols].astype(jnp.float32)
            ).astype(jnp.bfloat16)

        push(target, quads.at[z], q_send.at[k - 1], q_recv.at[z], {"seq": y * NZ + column[k]})

    for k in range(1, NZ):
        push(own_rows, own_rows, z_send.at[k - 1], z_recv.at[z], {"seq": y * NZ + column[k]})
    gather_send(0)
    gather_send(1)
    gather_pass(0)
    gather_send(2)
    gather_pass(1)
    compute(0)
    gather_send(3)
    gather_pass(2)
    compute(1)
    reduce_far(1)
    gather_pass(3)
    compute(2)
    reduce_far(2)
    reduce_near(1)
    compute(3)
    reduce_far(3)
    reduce_near(2)
    reduce_own(1)
    reduce_far(0)
    reduce_near(3)
    reduce_own(2)
    reduce_near(0)
    reduce_own(3)
    reduce_own(0)
    for k in range(1, NZ):
        arrive(quads.at[column[k]], q_send.at[k - 1], q_recv.at[column[k]])
    mine = part_block(0, y)

    @pl.loop(0, width // 512)
    def _(n):
        cols = pl.ds(pl.multiple_of(n * 512, 512), 512)
        total = (
            mine[:, cols].astype(jnp.float32)
            + sides[0, 0, :, cols].astype(jnp.float32)
            + sides[0, 1, :, cols].astype(jnp.float32)
        )
        for k in range(1, NZ):
            total = total + quads[column[k], :, cols].astype(jnp.float32)
        leaving[:, :, cols] = total.astype(jnp.bfloat16).reshape(EXP, CAP, 512)

    for d in range(1, EXP):
        other = (exp + d) % EXP
        push(leaving.at[other], back.at[exp], r_send.at[d - 1], r_recv.at[d - 1], {"exp": other})
    back[exp] = leaving[exp]
    for d in range(1, EXP):
        source = (exp + EXP - d) % EXP
        arrive(back.at[source], r_send.at[d - 1], r_recv.at[d - 1])
    result[...] = back[...].reshape(ROWS, width)
    for started in sent:
        started.wait_send()


def experts(going, w_in, w_out):
    width, ff = w_in.shape
    dma = pltpu.SemaphoreType.DMA
    b16 = jnp.bfloat16
    vmem = pltpu.VMEM
    return pl.pallas_call(
        moe_kernel,
        out_shape=jax.ShapeDtypeStruct((ROWS, width), b16),
        in_specs=[
            pl.BlockSpec(memory_space=pltpu.VMEM),
            pl.BlockSpec(memory_space=pl.ANY),
            pl.BlockSpec(memory_space=pl.ANY),
        ],
        out_specs=pl.BlockSpec(memory_space=pltpu.VMEM),
        scratch_shapes=[
            vmem((EXP, CAP, width), b16),
            vmem((NZ, NY * ROWS, width), b16),
            vmem((NY * ROWS, ff), b16),
            vmem((NZ, NY * ROWS, width), b16),
            vmem((NZ, 2, HALF, width), b16),
            vmem((NZ, 2, ROWS, width), b16),
            vmem((NZ, ROWS, width), b16),
            vmem((EXP, CAP, width), b16),
            vmem((EXP, CAP, width), b16),
            vmem((width, ff), b16),
            vmem((ff, width), b16),
            dma((2,)),
            dma((EXP - 1,)), dma((EXP - 1,)),
            dma((NZ - 1,)), dma((NZ,)),
            dma((NZ, 2)), dma((NZ, 2)),
            dma((NZ, 2)), dma((NZ, 2)),
            dma((NZ, 2)), dma((NZ, 2)),
            dma((NZ, 2)), dma((NZ, 2)),
            dma((NZ - 1,)), dma((NZ,)),
            dma((EXP - 1,)), dma((EXP - 1,)),
        ],
        compiler_params=pltpu.CompilerParams(
            collective_id=0, has_side_effects=True, vmem_limit_bytes=67043328
        ),
    )(going, w_in, w_out)


def shards(queries, keys, values, doc_ids, norm_gain, expert_ids, route_weights, w_in, w_out):
    block_len, heads_dev, head_dim = queries.shape
    seq_count = lax.axis_size("seq")
    exp_count = lax.axis_size("exp")
    seq_index = lax.axis_index("seq")
    reach_blocks = min(-(-WINDOW // block_len), seq_count - 1)
    all_keys, all_values = gather_context(keys[:, 0, :], values[:, 0, :])
    key_count = (reach_blocks + 1) * block_len
    key_start = jnp.maximum(seq_index - reach_blocks, 0) * block_len
    near_keys = lax.dynamic_slice_in_dim(all_keys, key_start, key_count, 0)
    near_values = lax.dynamic_slice_in_dim(all_values, key_start, key_count, 0)
    query_rows = jnp.transpose(queries, (1, 0, 2)).reshape(heads_dev * block_len, head_dim)
    score = lax.dot_general(
        query_rows, near_keys, (((1,), (1,)), ((), ())), preferred_element_type=jnp.float32
    )
    score = score * (1.0 / head_dim**0.5)
    query_pos = seq_index * block_len + jnp.arange(block_len, dtype=jnp.int32)
    key_pos = key_start + jnp.arange(key_count, dtype=jnp.int32)
    key_docs = lax.dynamic_slice_in_dim(doc_ids, key_start, key_count, 0)
    query_docs = lax.dynamic_slice_in_dim(doc_ids, seq_index * block_len, block_len, 0)
    allowed = (key_pos[None, :] <= query_pos[:, None]) & (
        query_pos[:, None] - key_pos[None, :] < WINDOW
    )
    allowed = allowed & (query_docs[:, None] == key_docs[None, :])
    allowed = jnp.tile(allowed, (heads_dev, 1))
    score = jnp.where(allowed, score, -jnp.inf)
    top_score = jnp.max(score, axis=1, keepdims=True)
    weights = jnp.where(allowed, jnp.exp(score - top_score), 0.0)
    probs = (weights / jnp.sum(weights, axis=1, keepdims=True)).astype(jnp.bfloat16)
    attended = jnp.dot(probs, near_values, preferred_element_type=jnp.float32).astype(jnp.bfloat16)
    attended = jnp.transpose(attended.reshape(heads_dev, block_len, head_dim), (1, 0, 2)).reshape(
        block_len, heads_dev * head_dim
    )
    attn = lax.all_to_all(attended, "exp", split_axis=0, concat_axis=1, tiled=True)
    token_count = attn.shape[0]
    width = attn.shape[1]
    attn_float = attn.astype(jnp.float32)
    mean_square = jnp.mean(attn_float * attn_float, axis=1, keepdims=True)
    normed = (attn_float * lax.rsqrt(mean_square + epsilon) * norm_gain[None, :]).astype(
        jnp.bfloat16
    )
    flat_ids = expert_ids.reshape(token_count * 2)
    onehot = (flat_ids[:, None] == jnp.arange(exp_count, dtype=jnp.int32)[None, :]).astype(
        jnp.int32
    )
    earlier = jnp.cumsum(onehot, axis=0) - onehot
    slot = jnp.sum(earlier * onehot, axis=1)
    local_code = (flat_ids * CAP + slot).reshape(token_count, 2)
    slot_range = jnp.arange(ROWS, dtype=jnp.int32)
    first_hit = local_code[:, 0:1] == slot_range[None, :]
    second_hit = local_code[:, 1:2] == slot_range[None, :]
    placing = jnp.transpose((first_hit | second_hit).astype(jnp.bfloat16))
    outgoing = jnp.dot(placing, normed, preferred_element_type=jnp.float32).astype(jnp.bfloat16)
    returned = experts(outgoing.reshape(EXP, CAP, width), w_in[0], w_out[0])
    combine = route_weights[:, 0:1] * first_hit.astype(jnp.float32) + route_weights[
        :, 1:2
    ] * second_hit.astype(jnp.float32)
    moe_part = jnp.dot(
        combine,
        returned.astype(jnp.float32),
        precision=lax.Precision.HIGHEST,
        preferred_element_type=jnp.float32,
    )
    return (attn_float + moe_part).astype(jnp.bfloat16)


def solution(mesh):
    placed = (
        P(("dp", "seq"), "exp", None),
        P(("dp", "seq"), "exp", None),
        P(("dp", "seq"), "exp", None),
        P("dp"),
        P(),
        P(("dp", "seq", "exp"), None),
        P(("dp", "seq", "exp"), None),
        P("exp", None, "seq"),
        P("exp", "seq", None),
    )
    return jax.shard_map(
        shards, mesh=mesh, in_specs=placed, out_specs=P(("dp", "seq", "exp"), None), check_vma=False
    )
```

```python
import functools

import jax
import jax.numpy as jnp
from jax import lax
from jax.experimental import pallas as pl
from jax.experimental.pallas import tpu as pltpu
from jax.sharding import PartitionSpec as P

WINDOW = 2048
EXP = 8
NY = 4
NZ = 4
CAP = 8
ROWS = EXP * CAP
HALF = ROWS // 2
TOK = 24
DIRECT = 3584

epsilon = 1e-05


def place_on_torus():
    seq = lax.axis_index("seq")
    y = seq // NZ
    z = seq % NZ
    column = [z, z + 1 - 2 * (z % 2), 2 - z // 2, 3 - 3 * (z // 2)]
    return y, z, column


def context_kernel(
    keys, values, info, all_keys, all_values, all_info, z_send, z_recv, y_send, y_recv, h_send, h_recv
):
    y, z, column = place_on_torus()
    y_up = (y + 1) % NY
    y_down = (y + NY - 1) % NY
    y_far = (y + 2) % NY
    up = {"seq": y_up * NZ + z}
    down = {"seq": y_down * NZ + z}
    length = {id(ref): own.shape[0] for own, ref in zip((keys, values, info), (all_keys, all_values, all_info))}

    barrier = pltpu.get_barrier_semaphore()
    greeted = [up, down] + [{"seq": y * NZ + column[k]} for k in range(1, NZ)]
    for device in greeted:
        pl.semaphore_signal(barrier, inc=1, device_id=device, device_id_type=pl.DeviceIdType.MESH)

    def rows_of(ref, col, yy):
        size = length[id(ref)]
        return ref.at[pl.ds(pl.multiple_of((yy * NZ + col) * size, size), size)]

    def half_of(ref, col, yy, h):
        size = length[id(ref)]
        half = size // 2
        start = (yy * NZ + col) * size + h * half
        return ref.at[pl.ds(pl.multiple_of(start, half), half)]

    both = (all_keys, all_values, all_info)
    for own, ref in zip((keys, values, info), both):
        rows_of(ref, z, y)[...] = own[...]
    pl.semaphore_wait(barrier, len(greeted))
    sent = []

    def copy(ref, send, recv, device):
        return pltpu.make_async_remote_copy(
            src_ref=ref, dst_ref=ref, send_sem=send, recv_sem=recv,
            device_id=device, device_id_type=pl.DeviceIdType.MESH,
        )

    def push(ref, send, recv, device):
        started = copy(ref, send, recv, device)
        started.start()
        sent.append(started)

    for k in range(1, NZ):
        for i, ref in enumerate(both):
            push(
                rows_of(ref, z, y), z_send.at[k - 1, i], z_recv.at[z, i],
                {"seq": y * NZ + column[k]},
            )

    def spread(k):
        for i, ref in enumerate(both):
            block = rows_of(ref, column[k], y)
            if k > 0:
                copy(block, z_send.at[k - 1, i], z_recv.at[column[k], i], up).wait_recv()
            push(block, y_send.at[k, 0, i], y_recv.at[k, 0, i], up)
            push(block, y_send.at[k, 1, i], y_recv.at[k, 1, i], down)

    def pass_on(k):
        for h, yy, device in ((0, y_down, up), (1, y_up, down)):
            for i, ref in enumerate(both):
                block = rows_of(ref, column[k], yy)
                copy(block, y_send.at[k, h, i], y_recv.at[k, h, i], up).wait_recv()
                part = half_of(ref, column[k], yy, h)
                push(part, h_send.at[k, h, i], h_recv.at[k, h, i], device)

    spread(0)
    spread(1)
    pass_on(0)
    spread(2)
    pass_on(1)
    spread(3)
    pass_on(2)
    pass_on(3)
    for k in range(NZ):
        for h in range(2):
            for i, ref in enumerate(both):
                part = half_of(ref, column[k], y_far, h)
                copy(part, h_send.at[k, h, i], h_recv.at[k, h, i], up).wait_recv()
    for started in sent:
        started.wait_send()


def gather_context(keys, values, info):
    length, head_dim = keys.shape
    dma = pltpu.SemaphoreType.DMA
    whole = jax.ShapeDtypeStruct((NY * NZ * length, head_dim), keys.dtype)
    vmem = pl.BlockSpec(memory_space=pltpu.VMEM)
    return pl.pallas_call(
        context_kernel,
        out_shape=(
            whole, whole, jax.ShapeDtypeStruct((NY * NZ * info.shape[0], info.shape[1]), info.dtype)
        ),
        in_specs=[vmem, vmem, vmem],
        out_specs=(vmem, vmem, vmem),
        scratch_shapes=[
            dma((NZ - 1, 3)), dma((NZ, 3)),
            dma((NZ, 2, 3)), dma((NZ, 2, 3)),
            dma((NZ, 2, 3)), dma((NZ, 2, 3)),
        ],
        compiler_params=pltpu.CompilerParams(collective_id=1, has_side_effects=True),
    )(keys, values, info)


def moe_kernel(
    going, tokens, place, pick, scale, w_in, w_out, result, result_far,
    arrived, rows, hidden, part, halves, sides, quads, leaving, back, wi, wo,
    tok, staged, landed, rows_far, homed, tpart, thalves, tsides, tquads,
    w_sem, x_send, x_recv, z_send, z_recv, y_send, y_recv, h_send, h_recv,
    a_send, a_recv, b_send, b_recv, q_send, q_recv, r_send, r_recv,
    tz_send, tz_recv, ty_send, ty_recv, th_send, th_recv, tx_send, tx_recv,
    tr_send, tr_recv, ta_send, ta_recv, tb_send, tb_recv, tq_send, tq_recv,
):
    exp = lax.axis_index("exp")
    y, z, column = place_on_torus()
    y_up = (y + 1) % NY
    y_down = (y + NY - 1) % NY
    y_far = (y + 2) % NY
    up = {"seq": y_up * NZ + z}
    down = {"seq": y_down * NZ + z}
    near = rows.shape[2]
    far = tok.shape[4]
    f32 = jnp.float32
    b16 = jnp.bfloat16

    load_in = pltpu.make_async_copy(w_in, wi, w_sem.at[0])
    load_out = pltpu.make_async_copy(w_out, wo, w_sem.at[1])
    load_in.start()
    load_out.start()

    barrier = pltpu.get_barrier_semaphore()
    greeted = [up, down]
    greeted += [{"seq": y * NZ + column[k]} for k in range(1, NZ)]
    greeted += [{"exp": (exp + d) % EXP} for d in range(1, EXP)]
    for device in greeted:
        pl.semaphore_signal(barrier, inc=1, device_id=device, device_id_type=pl.DeviceIdType.MESH)
    tok[z, y] = tokens[...]
    pl.semaphore_wait(barrier, len(greeted))

    sent = []

    def copy(src, dst, send, recv, device):
        return pltpu.make_async_remote_copy(
            src_ref=src, dst_ref=dst, send_sem=send, recv_sem=recv,
            device_id=device, device_id_type=pl.DeviceIdType.MESH,
        )

    def push(src, dst, send, recv, device, keep=sent):
        started = copy(src, dst, send, recv, device)
        started.start()
        keep.append(started)

    def arrive(dst, send, recv):
        copy(dst, dst, send, recv, up).wait_recv()

    def tiles(ref, size, body):
        @pl.loop(0, ref.shape[-1] // size)
        def _(n):
            body(pl.ds(pl.multiple_of(n * size, size), size))

    def block(col, yy):
        return rows.at[col, pl.ds(pl.multiple_of(yy * ROWS, ROWS), ROWS)]

    def half_block(col, yy, h):
        return rows.at[col, pl.ds(pl.multiple_of(yy * ROWS + h * HALF, HALF), HALF)]

    def part_block(k, yy):
        return part.at[k, pl.ds(pl.multiple_of(yy * ROWS, ROWS), ROWS)]

    def part_half(k, yy, h):
        return part.at[k, pl.ds(pl.multiple_of(yy * ROWS + h * HALF, HALF), HALF)]

    def far_half(h):
        return pl.ds(h * (far // 2), far // 2)

    def token_send(k):
        ref = tok.at[column[k], y]
        if k > 0:
            arrive(ref, tz_send.at[k - 1], tz_recv.at[column[k]])
        push(ref, ref, ty_send.at[k, 0], ty_recv.at[k, 0], up)
        push(ref, ref, ty_send.at[k, 1], ty_recv.at[k, 1], down)

    def token_pass(k):
        for h, yy, device in ((0, y_down, up), (1, y_up, down)):
            whole = tok.at[column[k], yy]
            arrive(whole, ty_send.at[k, h], ty_recv.at[k, h])
            ref = tok.at[column[k], yy, :, :, far_half(h)]
            push(ref, ref, th_send.at[k, h], th_recv.at[k, h], device)

    stage_sent = [[] for _ in range(NZ)]

    def token_place(k):
        for h in range(2):
            ref = tok.at[column[k], y_far, :, :, far_half(h)]
            arrive(ref, th_send.at[k, h], th_recv.at[k, h])

        @pl.loop(0, NY)
        def _(yy):
            chosen = place[yy * NZ + column[k]]

            def body(cols):
                held = tok[column[k], yy, :, :, cols].astype(f32).reshape(TOK, 512).astype(b16)
                put = jnp.dot(chosen, held, preferred_element_type=f32)
                staged[k, yy, :, :, cols] = put.reshape(EXP, CAP, 512).astype(b16)

            tiles(tok, 512, body)

        for d in range(1, EXP):
            other = (exp + d) % EXP
            push(
                staged.at[k, :, other], landed.at[k, :, exp],
                tx_send.at[k, d - 1], tx_recv.at[k, d - 1], {"exp": other}, stage_sent[k],
            )
        landed[k, :, exp] = staged[k, :, exp]

    for k in range(1, NZ):
        ref = tok.at[z, y]
        push(ref, ref, tz_send.at[k - 1], tz_recv.at[z], {"seq": y * NZ + column[k]})
    token_send(0)

    for d in range(1, EXP):
        other = (exp + d) % EXP
        push(going.at[other], arrived.at[exp], x_send.at[d - 1], x_recv.at[d - 1], {"exp": other})
    arrived[exp] = going[exp]
    token_send(1)
    token_pass(0)
    token_send(2)
    token_pass(1)
    token_send(3)
    token_pass(2)
    token_pass(3)
    for d in range(1, EXP):
        source = (exp + EXP - d) % EXP
        arrive(arrived.at[source], x_send.at[d - 1], x_recv.at[d - 1])
    own_rows = block(z, y)
    own_rows[...] = arrived[...].reshape(ROWS, near)

    def gather_send(k):
        ref = block(column[k], y)
        if k > 0:
            arrive(ref, z_send.at[k - 1], z_recv.at[column[k]])
        push(ref, ref, y_send.at[k, 0], y_recv.at[k, 0], up)
        push(ref, ref, y_send.at[k, 1], y_recv.at[k, 1], down)

    def gather_pass(k):
        for h, yy, device in ((0, y_down, up), (1, y_up, down)):
            arrive(block(column[k], yy), y_send.at[k, h], y_recv.at[k, h])
            ref = half_block(column[k], yy, h)
            push(ref, ref, h_send.at[k, h], h_recv.at[k, h], device)

    def compute(k):
        for d in range(1, EXP):
            source = (exp + EXP - d) % EXP
            arrive(landed.at[k, :, source], tx_send.at[k, d - 1], tx_recv.at[k, d - 1])

        def gather_far(cols):
            rows_far[:, cols] = (
                landed[k, :, :, :, cols].astype(f32).reshape(NY * ROWS, 512).astype(b16)
            )

        tiles(rows_far, 512, gather_far)
        for h in range(2):
            arrive(half_block(column[k], y_far, h), h_send.at[k, h], h_recv.at[k, h])
        if k == 0:
            load_in.wait()
        rows_now = rows.at[column[k]]

        def first(cols):
            v = jnp.dot(rows_now[...], wi[:near, cols], preferred_element_type=f32)
            v = v + jnp.dot(rows_far[...], wi[near:, cols], preferred_element_type=f32)
            hidden[:, cols] = (v / (1.0 + jnp.exp(-v))).astype(b16)

        tiles(hidden, 256, first)
        if k == 0:
            load_out.wait()
        for started in stage_sent[k]:
            started.wait_send()

        @pl.loop(0, far // 512)
        def _(n):
            cols = pl.ds(pl.multiple_of(n * 512, 512), 512)
            wide = pl.ds(pl.multiple_of(near + n * 512, 512), 512)
            out = jnp.dot(hidden[...], wo[:, wide], preferred_element_type=f32)
            staged[k, :, :, :, cols] = out.reshape(NY, EXP, CAP, 512).astype(b16)

        for d in range(1, EXP):
            other = (exp + d) % EXP
            push(
                staged.at[k, :, other], homed.at[k, :, exp],
                tr_send.at[k, d - 1], tr_recv.at[k, d - 1], {"exp": other},
            )
        homed[k, :, exp] = staged[k, :, exp]

        def second(cols):
            part[k, :, cols] = jnp.dot(hidden[...], wo[:, cols], preferred_element_type=f32).astype(b16)

        tiles(part, 512, second)

    def reduce_far(k):
        push(part_half(k, y_far, 0), halves.at[k, 0], a_send.at[k, 0], a_recv.at[k, 0], up)
        push(part_half(k, y_far, 1), halves.at[k, 1], a_send.at[k, 1], a_recv.at[k, 1], down)

    def reduce_near(k):
        for h, yy, device in ((0, y_up, up), (1, y_down, down)):
            arrive(halves.at[k, h], a_send.at[k, h], a_recv.at[k, h])
            target = part_half(k, yy, h)

            def body(cols):
                target[:, cols] = (
                    target[:, cols].astype(f32) + halves[k, h, :, cols].astype(f32)
                ).astype(b16)

            tiles(part, 512, body)
            push(part_block(k, yy), sides.at[k, h], b_send.at[k, h], b_recv.at[k, h], device)

    def reduce_own(k):
        for h in range(2):
            arrive(sides.at[k, h], b_send.at[k, h], b_recv.at[k, h])
        if k == 0:
            return
        target = part_block(k, y)

        def body(cols):
            target[:, cols] = (
                target[:, cols].astype(f32)
                + sides[k, 0, :, cols].astype(f32)
                + sides[k, 1, :, cols].astype(f32)
            ).astype(b16)

        tiles(part, 512, body)
        push(target, quads.at[z], q_send.at[k - 1], q_recv.at[z], {"seq": y * NZ + column[k]})

    def token_mix(k):
        for d in range(1, EXP):
            source = (exp + EXP - d) % EXP
            arrive(homed.at[k, :, source], tr_send.at[k, d - 1], tr_recv.at[k, d - 1])

        @pl.loop(0, NY)
        def _(yy):
            chosen = pick[yy * NZ + column[k]]
            factor = scale[yy * NZ + column[k]]

            def body(cols):
                held = homed[k, yy, :, :, cols].astype(f32).reshape(ROWS, 512).astype(b16)
                got = jnp.dot(chosen, held, preferred_element_type=f32)
                mixed = got[:TOK] * factor[:, 0:1] + got[TOK:] * factor[:, 1:2]
                tpart[k, yy, :, :, cols] = mixed.reshape(TOK // 8, 8, 512).astype(b16)

            tiles(tpart, 512, body)

        for h, device in ((0, up), (1, down)):
            push(
                tpart.at[k, y_far, :, :, far_half(h)], thalves.at[k, h],
                ta_send.at[k, h], ta_recv.at[k, h], device,
            )

    def token_near(k):
        for h, yy, device in ((0, y_up, up), (1, y_down, down)):
            arrive(thalves.at[k, h], ta_send.at[k, h], ta_recv.at[k, h])
            tpart[k, yy, :, :, far_half(h)] = (
                tpart[k, yy, :, :, far_half(h)].astype(f32) + thalves[k, h].astype(f32)
            ).astype(b16)
            push(tpart.at[k, yy], tsides.at[k, h], tb_send.at[k, h], tb_recv.at[k, h], device)

    def token_own(k):
        for h in range(2):
            arrive(tsides.at[k, h], tb_send.at[k, h], tb_recv.at[k, h])
        if k == 0:
            return
        tpart[k, y] = (
            tpart[k, y].astype(f32) + tsides[k, 0].astype(f32) + tsides[k, 1].astype(f32)
        ).astype(b16)
        push(
            tpart.at[k, y], tquads.at[z], tq_send.at[k - 1], tq_recv.at[z],
            {"seq": y * NZ + column[k]},
        )

    for k in range(1, NZ):
        push(own_rows, own_rows, z_send.at[k - 1], z_recv.at[z], {"seq": y * NZ + column[k]})
    gather_send(0)
    for k in range(NZ):
        token_place(k)
    gather_send(1)
    gather_pass(0)
    gather_pass(1)
    gather_send(2)
    compute(0)
    gather_pass(2)
    gather_send(3)
    compute(1)
    reduce_far(1)
    gather_pass(3)
    compute(2)
    reduce_far(2)
    reduce_near(1)
    compute(3)
    reduce_far(3)
    reduce_far(0)
    reduce_near(2)
    reduce_own(1)
    token_mix(0)
    reduce_near(3)
    reduce_near(0)
    token_mix(1)
    reduce_own(2)
    token_near(0)
    token_mix(2)
    token_near(1)
    reduce_own(3)
    token_mix(3)
    token_near(2)
    token_own(0)
    token_own(1)
    reduce_own(0)
    token_near(3)
    token_own(2)
    token_own(3)
    for k in range(1, NZ):
        arrive(quads.at[column[k]], q_send.at[k - 1], q_recv.at[column[k]])
    mine = part_block(0, y)

    def finish(cols):
        total = (
            mine[:, cols].astype(f32)
            + sides[0, 0, :, cols].astype(f32)
            + sides[0, 1, :, cols].astype(f32)
        )
        for k in range(1, NZ):
            total = total + quads[column[k], :, cols].astype(f32)
        leaving[:, :, cols] = total.astype(b16).reshape(EXP, CAP, 512)

    tiles(part, 512, finish)
    for d in range(1, EXP):
        other = (exp + d) % EXP
        push(leaving.at[other], back.at[exp], r_send.at[d - 1], r_recv.at[d - 1], {"exp": other})
    back[exp] = leaving[exp]
    for k in range(1, NZ):
        arrive(tquads.at[column[k]], tq_send.at[k - 1], tq_recv.at[column[k]])
    total = tpart[0, y].astype(f32) + tsides[0, 0].astype(f32) + tsides[0, 1].astype(f32)
    for k in range(1, NZ):
        total = total + tquads[column[k]].astype(f32)
    result_far[...] = total.reshape(TOK, far)
    for d in range(1, EXP):
        source = (exp + EXP - d) % EXP
        arrive(back.at[source], r_send.at[d - 1], r_recv.at[d - 1])
    result[...] = back[...].reshape(ROWS, near)
    for started in sent:
        started.wait_send()


def experts(going, tokens, place, pick, scale, w_in, w_out):
    width, ff = w_in.shape
    near = going.shape[2]
    far = width - near
    dma = pltpu.SemaphoreType.DMA
    b16 = jnp.bfloat16
    vmem = pltpu.VMEM
    inside = pl.BlockSpec(memory_space=pltpu.VMEM)
    outside = pl.BlockSpec(memory_space=pl.ANY)
    wide = (NZ, NY, EXP, CAP, far)
    eights = TOK // 8
    one, each, pair, peers = dma((NZ - 1,)), dma((NZ,)), dma((NZ, 2)), dma((EXP - 1,))
    all_peers = dma((NZ, EXP - 1))
    return pl.pallas_call(
        moe_kernel,
        out_shape=(
            jax.ShapeDtypeStruct((ROWS, near), b16), jax.ShapeDtypeStruct((TOK, far), jnp.float32)
        ),
        in_specs=[inside] * 5 + [outside] * 2,
        out_specs=(inside, inside),
        scratch_shapes=[
            vmem((EXP, CAP, near), b16),
            vmem((NZ, NY * ROWS, near), b16),
            vmem((NY * ROWS, ff), b16),
            vmem((NZ, NY * ROWS, near), b16),
            vmem((NZ, 2, HALF, near), b16),
            vmem((NZ, 2, ROWS, near), b16),
            vmem((NZ, ROWS, near), b16),
            vmem((EXP, CAP, near), b16),
            vmem((EXP, CAP, near), b16),
            vmem((width, ff), b16),
            vmem((ff, width), b16),
            vmem((NZ, NY, eights, 8, far), b16),
            vmem(wide, b16),
            vmem(wide, b16),
            vmem((NY * ROWS, far), b16),
            vmem(wide, b16),
            vmem((NZ, NY, eights, 8, far), b16),
            vmem((NZ, 2, eights, 8, far // 2), b16),
            vmem((NZ, 2, eights, 8, far), b16),
            vmem((NZ, eights, 8, far), b16),
            dma((2,)),
            peers, peers, one, each, pair, pair, pair, pair,
            pair, pair, pair, pair, one, each, peers, peers,
            one, each, pair, pair, pair, pair, all_peers, all_peers,
            all_peers, all_peers, pair, pair, pair, pair, one, each,
        ],
        compiler_params=pltpu.CompilerParams(
            collective_id=0, has_side_effects=True, vmem_limit_bytes=67043328
        ),
    )(going, tokens, place, pick, scale, w_in, w_out)


def shards(queries, keys, values, doc_ids, norm_gain, expert_ids, route_weights, w_in, w_out):
    block_len, heads_dev, head_dim = queries.shape
    seq_count = lax.axis_size("seq")
    exp_count = lax.axis_size("exp")
    seq_index = lax.axis_index("seq")
    reach_blocks = min(-(-WINDOW // block_len), seq_count - 1)
    flat_ids = expert_ids.reshape(TOK * 2)
    onehot = (flat_ids[:, None] == jnp.arange(exp_count, dtype=jnp.int32)[None, :]).astype(
        jnp.int32
    )
    earlier = jnp.cumsum(onehot, axis=0) - onehot
    slot = jnp.sum(earlier * onehot, axis=1)
    local_code = (flat_ids * CAP + slot).reshape(TOK, 2)
    info = jnp.concatenate([local_code.astype(jnp.float32).T, route_weights.T], axis=0)
    info = jnp.pad(info, ((0, 12), (0, 128 - TOK)))
    all_keys, all_values, all_info = gather_context(keys[:, 0, :], values[:, 0, :], info)
    all_info = all_info.reshape(seq_count, 16, 128)[:, :4, :TOK]
    all_codes = all_info[:, :2].astype(jnp.int32)
    slot_range = jnp.arange(ROWS, dtype=jnp.int32)
    hits = (all_codes[:, :, :, None] == slot_range).astype(jnp.bfloat16)
    pick = hits.reshape(seq_count, 2 * TOK, ROWS)
    place = jnp.transpose(hits[:, 0] + hits[:, 1], (0, 2, 1))
    scale = jnp.transpose(all_info[:, 2:], (0, 2, 1))
    key_count = (reach_blocks + 1) * block_len
    key_start = jnp.maximum(seq_index - reach_blocks, 0) * block_len
    near_keys = lax.dynamic_slice_in_dim(all_keys, key_start, key_count, 0)
    near_values = lax.dynamic_slice_in_dim(all_values, key_start, key_count, 0)
    query_rows = jnp.transpose(queries, (1, 0, 2)).reshape(heads_dev * block_len, head_dim)
    score = lax.dot_general(
        query_rows, near_keys, (((1,), (1,)), ((), ())), preferred_element_type=jnp.float32
    )
    score = score * (1.0 / head_dim**0.5)
    query_pos = seq_index * block_len + jnp.arange(block_len, dtype=jnp.int32)
    key_pos = key_start + jnp.arange(key_count, dtype=jnp.int32)
    key_docs = lax.dynamic_slice_in_dim(doc_ids, key_start, key_count, 0)
    query_docs = lax.dynamic_slice_in_dim(doc_ids, seq_index * block_len, block_len, 0)
    allowed = (key_pos[None, :] <= query_pos[:, None]) & (
        query_pos[:, None] - key_pos[None, :] < WINDOW
    )
    allowed = allowed & (query_docs[:, None] == key_docs[None, :])
    allowed = jnp.tile(allowed, (heads_dev, 1))
    score = jnp.where(allowed, score, -jnp.inf)
    top_score = jnp.max(score, axis=1, keepdims=True)
    weights = jnp.where(allowed, jnp.exp(score - top_score), 0.0)
    probs = (weights / jnp.sum(weights, axis=1, keepdims=True)).astype(jnp.bfloat16)
    attended = jnp.dot(probs, near_values, preferred_element_type=jnp.float32).astype(jnp.bfloat16)
    attended = jnp.transpose(attended.reshape(heads_dev, block_len, head_dim), (1, 0, 2)).reshape(
        block_len, heads_dev * head_dim
    )
    attn = lax.all_to_all(attended, "exp", split_axis=0, concat_axis=1, tiled=True)
    token_count = attn.shape[0]
    width = attn.shape[1]
    attn_float = attn.astype(jnp.float32)
    mean_square = jnp.mean(attn_float * attn_float, axis=1, keepdims=True)
    normed = (attn_float * lax.rsqrt(mean_square + epsilon) * norm_gain[None, :]).astype(
        jnp.bfloat16
    )
    first_hit = local_code[:, 0:1] == slot_range[None, :]
    second_hit = local_code[:, 1:2] == slot_range[None, :]
    placing = jnp.transpose((first_hit | second_hit).astype(jnp.bfloat16))
    outgoing = jnp.dot(
        placing, normed[:, :DIRECT], preferred_element_type=jnp.float32
    ).astype(jnp.bfloat16)
    returned, far_part = experts(
        outgoing.reshape(EXP, CAP, DIRECT),
        normed[:, DIRECT:].reshape(TOK // 8, 8, width - DIRECT),
        place, pick, scale, w_in[0], w_out[0],
    )
    combine = route_weights[:, 0:1] * first_hit.astype(jnp.float32) + route_weights[
        :, 1:2
    ] * second_hit.astype(jnp.float32)
    near_part = jnp.dot(
        combine,
        returned.astype(jnp.float32),
        precision=lax.Precision.HIGHEST,
        preferred_element_type=jnp.float32,
    )
    moe_part = jnp.concatenate([near_part, far_part], axis=1)
    return (attn_float + moe_part).astype(jnp.bfloat16)


def solution(mesh):
    placed = (
        P(("dp", "seq"), "exp", None),
        P(("dp", "seq"), "exp", None),
        P(("dp", "seq"), "exp", None),
        P("dp"),
        P(),
        P(("dp", "seq", "exp"), None),
        P(("dp", "seq", "exp"), None),
        P("exp", None, "seq"),
        P("exp", "seq", None),
    )
    return jax.shard_map(
        shards, mesh=mesh, in_specs=placed, out_specs=P(("dp", "seq", "exp"), None), check_vma=False
    )
```
